1024 devices in a mesh: dp: 16 (over x, y), proto: 64 (over z, core).
Axes of the slice: x: 4, y: 4, z: 32, core: 2. Of those that a mesh axis runs over, the one named last changes fastest.
Arguments:
- teacher_feat: bfloat16 [8192, 256], P('dp'), may hold values from -8 to 8
- small_feat: bfloat16 [8192, 256], P('dp'), may hold values from -6 to 6
- large_feat: bfloat16 [8192, 256], P('dp'), may hold values from -6 to 6
- teacher_proto: bfloat16 [256, 65536], P(None, 'proto'), may hold values from -4 to 4
- small_proto: bfloat16 [256, 65536], P(None, 'proto'), may hold values from -6 to 6
- large_proto: bfloat16 [256, 65536], P(None, 'proto'), may hold values from -6 to 6
Outputs:
- small_proto_grad: float32 [256, 65536], P('dp', 'proto')
- large_proto_grad: float32 [256, 65536], P('dp', 'proto')
- small_feat_grad: float32 [8192, 256], P('dp')
- large_feat_grad: float32 [8192, 256], P('dp')
The draws below stay inside these ranges and needn't reach their ends.
All inputs are finite; a program needn't handle non-finite values.
Results may differ from the reference program's by a relative error of at most 0.012.
The reference program's roundings to bfloat16 on the way count: a program that leaves them out, or rounds other values in their place, can miss the bound.
Values sent between devices are 32-bit elements; how exact they have to be, the bound alone decides.
A program may use at most 32 MiB of HBM per device.

```python
import jax
import jax.numpy as jnp
from jax import lax

BOT = 256
PROTOS = 65536
CROP_DEV = 512
ITERS = 3
CROPS = 8192
N_DP = 16


def shared_directions(key):
    proto_key = jax.random.fold_in(key, 11)
    directions = jnp.clip(jax.random.normal(proto_key, (BOT, PROTOS), jnp.float32), -4.0, 4.0)
    return directions


def draw_teacher_proto(key, part):
    return shared_directions(key).astype(jnp.bfloat16)


def draw_teacher_feat(key, part):
    directions = shared_directions(key)
    cluster_count = 256
    stride = PROTOS // cluster_count
    upper = jax.random.randint(jax.random.fold_in(key, 21), (CROPS,), 1, cluster_count + 1)
    middle = jax.random.randint(jax.random.fold_in(key, 22), (CROPS,), 1, upper + 1)
    picked = jax.random.randint(jax.random.fold_in(key, 23), (CROPS,), 0, middle)
    ordering = jax.random.permutation(jax.random.fold_in(key, 24), cluster_count)
    columns = jnp.take(ordering, picked) * stride
    centers = jnp.take(directions, columns, axis=1).T
    strength = jax.random.uniform(jax.random.fold_in(key, 25), (CROPS, 1), jnp.float32, 0.4, 1.5)
    noise = jnp.clip(jax.random.normal(jax.random.fold_in(key, 26), (CROPS, BOT), jnp.float32), -4.0, 4.0)
    return jnp.clip(strength * centers + noise, -8.0, 8.0).astype(jnp.bfloat16)


def spiked(values, own_key, source, target, shards_of, factor):
    def block_of(axis_at):
        return (jnp.arange(values.shape[axis_at]) // (values.shape[axis_at] // shards_of)).reshape((-1,) + (1,) * (values.ndim - 1 - axis_at))

    near = jax.random.permutation(own_key, shards_of)[block_of(target)]
    far = (block_of(target) + shards_of // 2) % shards_of
    return jnp.where((block_of(source) == near) | (block_of(source) == far), factor * values, values)


def shard_levels(own_key, shape, shards, low, high):
    def one(position, parts):
        draws = jax.random.uniform(jax.random.fold_in(jax.random.fold_in(own_key, 6), position), (parts,), jnp.float32, low / len(shards), high / len(shards))
        return jnp.repeat(jnp.exp(draws), shape[position] // parts).reshape((-1,) + (1,) * (len(shape) - position - 1))

    factor_of = one(*shards[0])
    for cut in shards[1:]:
        factor_of = factor_of * one(*cut)
    return factor_of


def scatter_about(own_key, extent, spread, limit, cuts=(), dtype=jnp.bfloat16):
    factor_of = shard_levels(own_key, extent, cuts, -0.22, 0.18) if cuts else 1.0
    drawn = jax.random.normal(own_key, extent, jnp.float32) * spread * factor_of
    return jnp.minimum(jnp.maximum(drawn, -limit), limit).astype(dtype)


def heavy_noise(own_key, extent, scale, reach, split, heavy, dtype=jnp.bfloat16):
    values = scale * jax.random.normal(own_key, extent, jnp.float32)
    if split:
        values = values * shard_levels(own_key, extent, split, -0.22, 0.18)
    return jnp.clip(spiked(values, jax.random.fold_in(own_key, 3), *heavy), -reach, reach).astype(dtype)


def setup_inputs(seed: int = 0) -> dict:
    splits = jax.random.split(jax.random.key(seed), 7)
    return {
        "teacher_feat": draw_teacher_feat(jax.random.fold_in(splits[6], 71), 0),
        "small_feat": heavy_noise(splits[1], (CROPS, BOT), 1.0, 6.0, ((0, 16),), (0, 1, 16, 2.0)),
        "large_feat": heavy_noise(splits[2], (CROPS, BOT), 1.0, 6.0, ((0, 16),), (0, 1, 16, 2.0)),
        "teacher_proto": draw_teacher_proto(jax.random.fold_in(splits[6], 71), 0),
        "small_proto": scatter_about(splits[4], (BOT, PROTOS), 1.0, 6.0, ((1, 64),)),
        "large_proto": scatter_about(splits[5], (BOT, PROTOS), 1.0, 6.0, ((1, 64),)),
    }


teacher_temp = 0.07
student_temp = 0.1
loss_scale = 4096.0

def unit_rows(features):
    values = features.astype(jnp.float32)
    inv_norm = lax.rsqrt(lax.optimization_barrier(jnp.sum(values * values, axis=1, keepdims=True)) + 1e-12)
    return (values * inv_norm, inv_norm)

def unit_columns(prototypes):
    values = prototypes.astype(jnp.float32)
    inv_norm = lax.rsqrt(lax.optimization_barrier(jnp.sum(values * values, axis=0, keepdims=True)) + 1e-12)
    return (values * inv_norm).astype(jnp.bfloat16)

def head_block(unit_f, inv_norm, columns, target):
    unit_b = unit_f.astype(jnp.bfloat16)
    expo = jnp.exp(jnp.dot(unit_b, columns, preferred_element_type=jnp.float32) / student_temp)
    totals = lax.optimization_barrier(jnp.sum(expo, axis=1, keepdims=True))
    grad_b = (loss_scale / student_temp * (expo / totals - target)).astype(jnp.bfloat16)
    proto_term = jnp.dot(unit_b.T, grad_b, preferred_element_type=jnp.float32)
    back = jnp.dot(grad_b, columns.T, preferred_element_type=jnp.float32)
    feat_grad = (back - unit_f * lax.optimization_barrier(jnp.sum(unit_f * back, axis=1, keepdims=True))) * inv_norm
    return (proto_term, feat_grad)

def reference(teacher_feat, small_feat, large_feat, teacher_proto, small_proto, large_proto):
    teacher_unit = unit_rows(teacher_feat)[0].astype(jnp.bfloat16)
    energy = jnp.exp(jnp.dot(teacher_unit, unit_columns(teacher_proto), preferred_element_type=jnp.float32) / teacher_temp)
    crop_scale = jnp.ones((CROPS,), jnp.float32)
    proto_scale = jnp.ones((PROTOS,), jnp.float32)
    for sweep_index in range(ITERS):
        proto_scale = 1.0 / jnp.dot(crop_scale, energy, precision=lax.Precision.HIGHEST)
        crop_scale = 1.0 / jnp.dot(energy, proto_scale, precision=lax.Precision.HIGHEST)
    small_f, small_inv = unit_rows(small_feat)
    large_f, large_inv = unit_rows(large_feat)
    small_cols = unit_columns(small_proto)
    large_cols = unit_columns(large_proto)
    blocks = (energy.reshape(N_DP, CROP_DEV, PROTOS), crop_scale.reshape(N_DP, CROP_DEV), small_f.reshape(N_DP, CROP_DEV, BOT), small_inv.reshape(N_DP, CROP_DEV, 1), large_f.reshape(N_DP, CROP_DEV, BOT), large_inv.reshape(N_DP, CROP_DEV, 1))

    def visit(carry, block):
        energy_b, crop_b, s_unit, s_inv, l_unit, l_inv = block
        target = crop_b[:, None] * energy_b * proto_scale[None, :]
        s_term, s_feat = head_block(s_unit, s_inv, small_cols, target)
        l_term, l_feat = head_block(l_unit, l_inv, large_cols, target)
        return ((carry[0] + s_term, carry[1] + l_term), (s_feat, l_feat))
    zeros = jnp.zeros((BOT, PROTOS), jnp.float32)
    (small_grad, large_grad), (small_feats, large_feats) = lax.scan(visit, (zeros, zeros), blocks)
    return (small_grad, large_grad, small_feats.reshape(CROPS, BOT), large_feats.reshape(CROPS, BOT))
```

```python
import jax
import jax.numpy as jnp
from jax import lax
from jax.experimental import pallas as pl
from jax.experimental.pallas import tpu as pltpu
from jax.sharding import PartitionSpec as P

MESH = pl.DeviceIdType.MESH
F32 = jnp.float32
BF16 = jnp.bfloat16

ITERS = 3
LOG2E = 1.4426950408889634
TEACHER_EXPONENT = LOG2E / 0.07
STUDENT_EXPONENT = LOG2E / 0.1
GRAD_SCALE = 4096.0 / 0.1

ROWS = 512
BOT = 256
COLS = 1024
TILE = 128
WIDE = 256
DP = 16
NZ = 32
CONTRACT_LAST = (((1,), (1,)), ((), ()))


def kernel(
    tf, sf, lf, tp, sp, lp,
    pgs_out, pgl_out, fgs_out, fgl_out,
    energy, expo_s, expo_l, cols_t, cols_s, cols_l,
    unit_t, unit_s, unit_l, unit_st, unit_lt, acc, grad_s, grad_l, inv_total_ref,
    dp_own, dp_got, win_own, win_got, far_own, far_got,
    tot_own, totw_got, totf_own, totf_got,
    back, core_got, rsw_own, rsw_got, rsf_own, rsf_got,
    fin, agf_got, half, other, pg, pg_got,
    dp_ss, dp_rs, win_ss, win_rs, far_ss, far_rs, core_ss, core_rs,
    rsw_ss, rsw_rs, rsf_ss, rsf_rs, agf_ss, agf_rs, agw_ss, agw_rs, fwd_ss, fwd_rs, pg_ss, pg_rs,
):
    dp = lax.axis_index("dp")
    pr = lax.axis_index("proto")
    x, y = lax.div(dp, 4), lax.rem(dp, 4)
    z, core = lax.div(pr, 2), lax.rem(pr, 2)

    def dp_peer(k):
        px = lax.rem(x + lax.div(k, 4), 4)
        py = lax.rem(y + lax.rem(k, 4), 4)
        return px * 4 + py

    def z_at(offset):
        return lax.rem(z + offset + NZ, NZ)

    def near(w):
        return w - 3 + lax.div(w + 5, 8)

    def far(f):
        return 8 * f - 12

    def remote(src, dst, ss, rs, to_dp, to_z, to_core):
        return pltpu.make_async_remote_copy(
            src_ref=src, dst_ref=dst, send_sem=ss, recv_sem=rs,
            device_id=(to_dp, to_z * 2 + to_core), device_id_type=MESH,
        )

    def each(lo, hi, make):
        def go(k, carry):
            make(k).start()
            return carry
        lax.fori_loop(lo, hi, go, 0)

    def settle(lo, hi, make):
        def go(k, carry):
            make(k).wait()
            return carry
        lax.fori_loop(lo, hi, go, 0)

    barrier = pltpu.get_barrier_semaphore()

    def greet(to_dp, to_z, to_core):
        pl.semaphore_signal(
            barrier, inc=1, device_id=(to_dp, to_z * 2 + to_core), device_id_type=MESH
        )

    for offset in (-12, 12, -4, 4):
        greet(dp, z_at(offset), core)
        greet(dp, z_at(offset), 1 - core)
    for offset in (-3, 3, -2, 2, -1, 1):
        greet(dp, z_at(offset), core)
    greet(dp, z, 1 - core)
    for k in range(1, DP):
        greet(dp_peer(k), z, core)

    def units(feat, unit, unit_tr):
        for b in range(0, ROWS, TILE):
            v = feat[b : b + TILE, :].astype(F32)
            u = v * lax.rsqrt(jnp.sum(v * v, axis=1, keepdims=True) + 1e-12)
            unit[b : b + TILE, :] = u.astype(BF16)
            if unit_tr is not None:
                unit_tr[:, b : b + TILE] = u.T.astype(BF16)

    def head(unit, proto, cols, expo, exponent, finish):
        @pl.loop(0, COLS // WIDE)
        def _(j):
            at = pl.ds(pl.multiple_of(j * WIDE, WIDE), WIDE)
            v = proto[:, at].astype(F32)
            c = (v * lax.rsqrt(jnp.sum(v * v, axis=0, keepdims=True) + 1e-12)).astype(BF16)
            cols[:, at] = c
            e = jnp.exp2(jnp.dot(unit[...], c, preferred_element_type=F32) * exponent)
            expo[:, at] = e
            finish(at, e)

    def lane_sums(read, write):
        for b in range(0, ROWS, TILE):
            write(b, jnp.sum(read(b).T, axis=0, keepdims=True))

    def spread(row):
        return jnp.broadcast_to(row, (TILE, TILE)).T

    units(tf, unit_t, None)

    def teacher_finish(at, e):
        dp_own[0, :, at] = jnp.sum(e, axis=0, keepdims=True)

    head(unit_t, tp, cols_t, energy, TEACHER_EXPONENT, teacher_finish)

    def student_finish(at, e):
        acc[...] += e[:, :TILE] + e[:, TILE:]

    for which, (feat, unit, unit_tr, proto, cols, expo) in enumerate(
        ((sf, unit_s, unit_st, sp, cols_s, expo_s), (lf, unit_l, unit_lt, lp, cols_l, expo_l))
    ):
        units(feat, unit, unit_tr)
        acc[...] = jnp.zeros_like(acc)
        head(unit, proto, cols, expo, STUDENT_EXPONENT, student_finish)

        def put(b, row, which=which):
            tot_own[:, which * ROWS + b : which * ROWS + b + TILE] = row

        lane_sums(lambda b: acc[b : b + TILE, :], put)

    pl.semaphore_wait(barrier, 30)

    def tot_window(w):
        return remote(tot_own, totw_got.at[w], win_ss.at[3, w], win_rs.at[3, w], dp, z_at(near(w)), core)

    def tot_far(g):
        f, to_core = lax.div(g, 2), lax.rem(g, 2)
        return remote(
            totf_own, totf_got.at[f * 2 + core], far_ss.at[3, g], far_rs.at[3, f * 2 + core],
            dp, z_at(far(f)), to_core,
        )

    def tot_far_here(g):
        f = lax.div(g, 2)
        return remote(
            totf_own, totf_got.at[g], far_ss.at[3, g], far_rs.at[3, g], dp, z_at(far(f)), lax.rem(g, 2)
        )

    for it in range(ITERS):
        def dp_copy(k, it=it):
            return remote(dp_own.at[it], dp_got.at[it, k], dp_ss.at[it, k], dp_rs.at[it, k], dp_peer(k), z, core)

        def window(w, it=it):
            return remote(win_own.at[it], win_got.at[it, w], win_ss.at[it, w], win_rs.at[it, w], dp, z_at(near(w)), core)

        def far_send(g, it=it):
            f, to_core = lax.div(g, 2), lax.rem(g, 2)
            return remote(
                far_own.at[it], far_got.at[it, f * 2 + core], far_ss.at[it, g], far_rs.at[it, f * 2 + core],
                dp, z_at(far(f)), to_core,
            )

        def far_here(g, it=it):
            f = lax.div(g, 2)
            return remote(
                far_own.at[it], far_got.at[it, g], far_ss.at[it, g], far_rs.at[it, g],
                dp, z_at(far(f)), lax.rem(g, 2),
            )

        each(1, DP, dp_copy)
        settle(1, DP, dp_copy)
        col_total = dp_own[it]
        for k in range(1, DP):
            col_total += dp_got[it, k]
        proto_scale = 1.0 / col_total
        for b in range(0, ROWS, TILE):
            part = energy[b : b + TILE, :TILE] * proto_scale[:, :TILE]
            for c in range(TILE, COLS, TILE):
                part += energy[b : b + TILE, c : c + TILE] * proto_scale[:, c : c + TILE]
            win_own[it, :, b : b + TILE] = jnp.sum(part.T, axis=0, keepdims=True)
        each(0, 7, window)
        if it == 0:
            each(0, 7, tot_window)
        settle(0, 7, window)
        near_total = win_own[it]
        for w in range(7):
            near_total += win_got[it, w]
        far_own[it] = near_total
        each(0, 8, far_send)
        if it == 0:
            settle(0, 7, tot_window)
            tot_near = tot_own[...]
            for w in range(7):
                tot_near += totw_got[w]
            totf_own[...] = tot_near
            each(0, 8, tot_far)
        settle(0, 8, far_here)
        row_total = far_got[it, 0]
        for g in range(1, 8):
            row_total += far_got[it, g]
        crop_scale = 1.0 / row_total
        if it < ITERS - 1:
            sums = [None] * (COLS // TILE)
            for b in range(0, ROWS, TILE):
                along = spread(crop_scale[:, b : b + TILE])
                for c in range(COLS // TILE):
                    part = jnp.sum(
                        along * energy[b : b + TILE, c * TILE : (c + 1) * TILE], axis=0, keepdims=True
                    )
                    sums[c] = part if sums[c] is None else sums[c] + part
            for c in range(COLS // TILE):
                dp_own[it + 1, :, c * TILE : (c + 1) * TILE] = sums[c]

    settle(0, 8, tot_far_here)
    total = totf_got[0]
    for g in range(1, 8):
        total += totf_got[g]
    inv_total_ref[...] = GRAD_SCALE / total
    inv_total = inv_total_ref[...]
    proto_grad_scale = proto_scale * GRAD_SCALE

    for b in range(0, ROWS, TILE):
        along = spread(crop_scale[:, b : b + TILE])
        small_along = spread(inv_total[:, b : b + TILE])
        large_along = spread(inv_total[:, ROWS + b : ROWS + b + TILE])
        for c in range(0, COLS, TILE):
            target = along * energy[b : b + TILE, c : c + TILE] * proto_grad_scale[:, c : c + TILE]
            grad_s[b : b + TILE, c : c + TILE] = (
                expo_s[b : b + TILE, c : c + TILE] * small_along - target
            ).astype(BF16)
            grad_l[b : b + TILE, c : c + TILE] = (
                expo_l[b : b + TILE, c : c + TILE] * large_along - target
            ).astype(BF16)

    half_rows = ROWS // 2
    for i, (grad, cols) in enumerate(((grad_s, cols_s), (grad_l, cols_l))):
        back[:, i * BOT : (i + 1) * BOT] = lax.dot_general(
            grad[...], cols[...], CONTRACT_LAST, preferred_element_type=F32
        )
    mine = pl.multiple_of(core * half_rows, half_rows)
    theirs = pl.multiple_of((1 - core) * half_rows, half_rows)
    to_pair = remote(back.at[pl.ds(theirs, half_rows)], core_got, core_ss.at[0], core_rs.at[0], dp, z, 1 - core)
    to_pair.start()

    for i, (unit_tr, grad) in enumerate(((unit_st, grad_s), (unit_lt, grad_l))):
        for c in range(0, COLS, WIDE):
            pg[:, :, i * COLS + c : i * COLS + c + WIDE] = jnp.dot(
                unit_tr[...], grad[:, c : c + WIDE], preferred_element_type=F32
            ).reshape(DP, BOT // DP, WIDE)

    def pg_copy(k):
        to = dp_peer(k)
        return remote(pg.at[to], pg_got.at[k], pg_ss.at[k], pg_rs.at[k], to, z, core)

    to_pair.wait()

    @pl.loop(0, half_rows // 32)
    def _(i):
        rows = pl.ds(pl.multiple_of(i * 32, 32), 32)
        rsw_own[rows, :] = back[pl.ds(pl.multiple_of(mine + i * 32, 32), 32), :] + core_got[rows, :]

    def class_rows(of_z):
        return pl.ds(pl.multiple_of(lax.rem(of_z + 4, 8) * 32, 32), 32)

    def rs_window(w):
        to_z = z_at(near(w))
        return remote(rsw_own.at[class_rows(to_z)], rsw_got.at[w], rsw_ss.at[w], rsw_rs.at[w], dp, to_z, core)

    each(0, 7, rs_window)
    each(1, DP, pg_copy)
    settle(0, 7, rs_window)
    window_sum = rsw_own[class_rows(z), :]
    for w in range(7):
        window_sum += rsw_got[w]
    rsf_own[...] = window_sum

    def owner_rows(of_z):
        return pl.ds(pl.multiple_of(lax.div(of_z, 8) * 8, 8), 8)

    def rs_far(f):
        to_z = z_at(far(f))
        return remote(rsf_own.at[owner_rows(to_z)], rsf_got.at[f], rsf_ss.at[f], rsf_rs.at[f], dp, to_z, core)

    each(0, 4, rs_far)
    settle(0, 4, rs_far)
    own_back = (rsf_got[0] + rsf_got[1]) + (rsf_got[2] + rsf_got[3])

    first = pl.multiple_of(mine + lax.rem(z, 8) * 32 + lax.div(z, 8) * 8, 8)
    for i, feat in enumerate((sf, lf)):
        v = feat[pl.ds(first, 8), :].astype(F32)
        inv = lax.rsqrt(jnp.sum(v * v, axis=1, keepdims=True) + 1e-12)
        u = v * inv
        b = own_back[:, i * BOT : (i + 1) * BOT]
        fin[:, i * BOT : (i + 1) * BOT] = (b - u * jnp.sum(u * b, axis=1, keepdims=True)) * inv

    def ag_far(f):
        return remote(fin, agf_got.at[owner_rows(z)], agf_ss.at[f], agf_rs.at[f], dp, z_at(far(f)), core)

    def ag_far_here(f):
        return remote(
            fin, agf_got.at[owner_rows(z_at(-far(f)))], agf_ss.at[f], agf_rs.at[f], dp, z_at(far(f)), core
        )

    each(0, 4, ag_far)
    settle(0, 4, ag_far_here)

    def ag_window(w):
        return remote(agf_got, half.at[w], agw_ss.at[w], agw_rs.at[w], dp, z_at(-near(w)), core)

    each(0, 7, ag_window)

    def ag_pair(w):
        return remote(half.at[w], other.at[w], fwd_ss.at[w], fwd_rs.at[w], dp, z, 1 - core)

    own_pair = remote(agf_got, other.at[7], fwd_ss.at[7], fwd_rs.at[7], dp, z, 1 - core)
    own_pair.start()

    def put_rows(from_z, base, value):
        rows = pl.ds(pl.multiple_of(base + lax.rem(from_z + 4, 8) * 32, 32), 32)
        fgs_out[rows, :] = value[:, :BOT]
        fgl_out[rows, :] = value[:, BOT:]

    put_rows(z, mine, agf_got[...])

    settle(1, DP, pg_copy)
    pg_total = pg[dp]
    for k in range(1, DP):
        pg_total += pg_got[k]
    pgs_out[...] = pg_total[:, :COLS]
    pgl_out[...] = pg_total[:, COLS:]

    for w in (2, 3, 1, 4, 0, 5, 6):
        ag_window(w).wait()
        ag_pair(w).start()
        put_rows(z_at(near(w)), mine, half[w])
    own_pair.wait()
    put_rows(z, theirs, other[7])
    for w in (2, 3, 1, 4, 0, 5, 6):
        ag_pair(w).wait()
        put_rows(z_at(near(w)), theirs, other[w])


def on_device(*args):
    dma = pltpu.SemaphoreType.DMA
    vmem = pltpu.VMEM
    pairs = lambda *shape: [dma(shape), dma(shape)]
    return pl.pallas_call(
        kernel,
        out_shape=(
            jax.ShapeDtypeStruct((BOT // DP, COLS), F32),
            jax.ShapeDtypeStruct((BOT // DP, COLS), F32),
            jax.ShapeDtypeStruct((ROWS, BOT), F32),
            jax.ShapeDtypeStruct((ROWS, BOT), F32),
        ),
        in_specs=[pl.BlockSpec(memory_space=vmem)] * 6,
        out_specs=(pl.BlockSpec(memory_space=vmem),) * 4,
        scratch_shapes=[
            vmem((ROWS, COLS), F32), vmem((ROWS, COLS), F32), vmem((ROWS, COLS), F32),
            vmem((BOT, COLS), BF16), vmem((BOT, COLS), BF16), vmem((BOT, COLS), BF16),
            vmem((ROWS, BOT), BF16), vmem((ROWS, BOT), BF16), vmem((ROWS, BOT), BF16),
            vmem((BOT, ROWS), BF16), vmem((BOT, ROWS), BF16),
            vmem((ROWS, TILE), F32),
            vmem((ROWS, COLS), BF16), vmem((ROWS, COLS), BF16),
            vmem((1, 2 * ROWS), F32),
            vmem((ITERS, 1, COLS), F32), vmem((ITERS, DP, 1, COLS), F32),
            vmem((ITERS, 1, ROWS), F32), vmem((ITERS, 7, 1, ROWS), F32),
            vmem((ITERS, 1, ROWS), F32), vmem((ITERS, 8, 1, ROWS), F32),
            vmem((1, 2 * ROWS), F32), vmem((7, 1, 2 * ROWS), F32),
            vmem((1, 2 * ROWS), F32), vmem((8, 1, 2 * ROWS), F32),
            vmem((ROWS, 2 * BOT), F32), vmem((ROWS // 2, 2 * BOT), F32),
            vmem((ROWS // 2, 2 * BOT), F32), vmem((7, 32, 2 * BOT), F32),
            vmem((32, 2 * BOT), F32), vmem((4, 8, 2 * BOT), F32),
            vmem((8, 2 * BOT), F32), vmem((32, 2 * BOT), F32),
            vmem((7, 32, 2 * BOT), F32), vmem((8, 32, 2 * BOT), F32),
            vmem((DP, BOT // DP, 2 * COLS), F32), vmem((DP, BOT // DP, 2 * COLS), F32),
            *pairs(ITERS, DP), *pairs(ITERS + 1, 7), *pairs(ITERS + 1, 8), *pairs(1),
            *pairs(7), *pairs(4), *pairs(4), *pairs(7), *pairs(8), *pairs(DP),
        ],
        compiler_params=pltpu.CompilerParams(
            collective_id=0, has_side_effects=True, vmem_limit_bytes=56 * 1024 * 1024
        ),
        name="sinkhorn_step",
    )(*args)


def solution(mesh):
    placed = (
        P("dp", None), P("dp", None), P("dp", None),
        P(None, "proto"), P(None, "proto"), P(None, "proto"),
    )
    return jax.shard_map(
        on_device,
        mesh=mesh,
        in_specs=placed,
        out_specs=(P("dp", "proto"), P("dp", "proto"), P("dp", None), P("dp", None)),
        check_vma=False,
    )
```
